32 devices in a mesh: blk: 8 (over z, x), lane: 4 (over y, core).
Axes of the slice: x: 2, y: 2, z: 4, core: 2. Of those that a mesh axis runs over, the one named last changes fastest.
Arguments:
- features: float32 [12288, 512], P(('blk', 'lane')), may hold values from -6 to 6
- weight: float32 [512, 512], replicated, may hold values from -0.25 to 0.25
- hub_values: float32 [3, 12288, 1536], P(None, 'blk', 'lane'), may hold values from -0.125 to 0.125
- hub_mask: int32 [3, 96, 12], P(None, 'blk', 'lane'), may hold values 0 or 1
- tail_values: float32 [576, 128, 128], P(('blk', 'lane')), may hold values from -0.21875 to 0.21875
- tail_reader: int32 [576], P(('blk', 'lane')), may hold values from 0 to 7, as said below
- tail_target: int32 [576], P(('blk', 'lane')), may hold values from 0 to 2
Outputs:
- activations: float32 [12288, 512], P(('blk', 'lane'))
The draws below stay inside these ranges and needn't reach their ends.
Inputs may be any that keep to these rules, and one draw needn't show every extreme that they name: `tail_reader`: A tail tile of a device in slab b names a reader (b + o) mod 8 with 1 <= o <= 4; within one device's 18 tail tiles no reader is named more than 5 times, and on every device some reader is named exactly 5 times.
All inputs are finite; a program needn't handle non-finite values. No bound on the sum of `hub_mask` on one device may be relied on, other than what follows from the above.
Results may differ from the reference program's by a relative error of at most 0.0003.
Values sent between devices are 32-bit elements; how exact they have to be, the bound alone decides.
No kernel may reach another device: no remote copies, remote signals or barrier semaphores. Data moves between devices by JAX's collectives and lax.ppermute only.
A program may use at most 128 MiB of HBM per device.

```python
import jax
import jax.numpy as jnp
from jax import lax

FEAT = 512
BLOCK = 128
TILES = 6
STOPS = 3
BLOCKS = 3
TAILS = 18
REACH = 4
SLOT_CAP = 5
SLAB = 1536
VERTS = 12288
ALL_TILES = 576
N_BLK = 8
N_LANE = 4


def draw_tail_reader(key, part):
    special = jax.random.randint(jax.random.fold_in(key, 7), (), 0, N_BLK * N_LANE).astype(jnp.int32)

    def one_device(device_id):
        dev_key = jax.random.fold_in(key, device_id)
        slab_idx = device_id // N_LANE
        hot_offset = jax.random.randint(jax.random.fold_in(dev_key, 1), (), 0, REACH).astype(jnp.int32)
        hot_offset = jnp.where(device_id == special, REACH - 1, hot_offset).astype(jnp.int32)
        others = jax.random.permutation(jax.random.fold_in(dev_key, 2), (REACH - 1) * SLOT_CAP)
        other_offset = (others // SLOT_CAP).astype(jnp.int32)
        other_offset = other_offset + (other_offset >= hot_offset).astype(jnp.int32)
        chosen = jnp.concatenate([jnp.full((SLOT_CAP,), hot_offset, jnp.int32), other_offset[:TAILS - SLOT_CAP]])
        chosen = jax.random.permutation(jax.random.fold_in(dev_key, 3), chosen)
        return ((slab_idx + 1 + chosen) % N_BLK).astype(jnp.int32)
    device_ids = jnp.arange(N_BLK * N_LANE, dtype=jnp.int32)
    return jax.vmap(one_device)(device_ids).reshape(-1).astype(jnp.int32)


def plant(array, key, smallest, top_value):
    spot = [jax.random.randint(jax.random.fold_in(key, axis), (), 0, length) for axis, length in enumerate(array.shape)]
    main_axis = array.shape.index(max(array.shape))
    next_to = spot[:main_axis] + [(spot[main_axis] + 1) % array.shape[main_axis]] + spot[main_axis + 1:]
    return array.at[tuple(spot)].set(smallest).at[tuple(next_to)].set(top_value)


def levels(own_key, shape, cuts, low, top_value):
    level = 1.0
    for position, blocks in cuts:
        heights = jax.random.uniform(jax.random.fold_in(jax.random.fold_in(own_key, 6), position), (blocks,), jnp.float32, low / len(cuts), top_value / len(cuts))
        level = level * jnp.repeat(jnp.exp(heights), shape[position] // blocks).reshape((-1,) + (1,) * (len(shape) - 1 - position))
    return level


def centred(stream_key, extent, deviation, reach, split=(), kind=jnp.bfloat16):
    result = jax.random.normal(stream_key, extent, jnp.float32) * deviation
    if len(split) > 0:
        result = levels(stream_key, extent, split, -0.22, 0.18) * result
    return jnp.clip(result, min=-reach, max=reach).astype(kind)


def setup_inputs(seed: int = 0) -> dict:
    key_of = jax.random.split(jax.random.key(seed), 8)
    features = centred(key_of[0], (VERTS, FEAT), 1.0, 6.0, ((0, 32),), jnp.float32)
    weight = centred(key_of[1], (FEAT, FEAT), FEAT ** -0.5, 0.25, (), jnp.float32)
    hub_values = centred(key_of[2], (STOPS, VERTS, SLAB), (STOPS * SLAB // 2) ** -0.5, 0.125, ((1, 8), (2, 4)), jnp.float32)
    hub_mask = plant((jax.random.randint(key_of[3], (STOPS, VERTS // BLOCK, SLAB // BLOCK), 0, 2) < 1).astype(jnp.int32), jax.random.fold_in(key_of[3], 1), 0, 1)
    tail_values = centred(key_of[4], (ALL_TILES, BLOCK, BLOCK), (BLOCK * TILES) ** -0.5, 0.21875, ((0, 32),), jnp.float32)
    tail_reader = draw_tail_reader(jax.random.fold_in(key_of[7], 71), 0)
    tail_target = plant(jax.random.randint(key_of[6], (ALL_TILES,), 0, BLOCKS), jax.random.fold_in(key_of[6], 1), 0, BLOCKS - 1).astype(jnp.int32)
    return dict(features=features, weight=weight, hub_values=hub_values, hub_mask=hub_mask, tail_values=tail_values, tail_reader=tail_reader, tail_target=tail_target)


def reference(features, weight, hub_values, hub_mask, tail_values, tail_reader, tail_target):
    highest = lax.Precision.HIGHEST
    slabs = features.reshape(N_BLK, SLAB, FEAT)
    tile_rows = SLAB // BLOCK

    def one_slab(slab_idx):
        running = jnp.zeros((SLAB, FEAT), jnp.float32)
        for stop_idx in range(STOPS):
            hub_slice = lax.dynamic_slice_in_dim(hub_values[stop_idx], slab_idx * SLAB, SLAB, 0)
            mask_slice = lax.dynamic_slice_in_dim(hub_mask[stop_idx], slab_idx * tile_rows, tile_rows, 0)
            expanded = jnp.repeat(jnp.repeat(mask_slice.astype(jnp.float32), BLOCK, 0), BLOCK, 1)
            source = slabs[(slab_idx - stop_idx) % N_BLK]
            running = running + jnp.dot(hub_slice * expanded, source, precision=highest, preferred_element_type=jnp.float32)
        return running

    hub_agg = lax.map(one_slab, jnp.arange(N_BLK, dtype=jnp.int32)).reshape(VERTS, FEAT)

    device_total = N_BLK * N_LANE
    block_feats = features.reshape(device_total, BLOCKS, BLOCK, FEAT)
    tile_vals = tail_values.reshape(device_total, BLOCKS, TILES, BLOCK, BLOCK)

    def device_products(pair):
        return jnp.einsum("kjab,kbf->kjaf", pair[0], pair[1], precision=highest)

    products = lax.map(device_products, (tile_vals, block_feats))
    device_ids = jnp.arange(device_total, dtype=jnp.int32)[:, None]
    lane_ids = device_ids % N_LANE
    readers = tail_reader.reshape(device_total, TAILS)
    targets = tail_target.reshape(device_total, TAILS)
    dest_block = ((readers * N_LANE + lane_ids) * BLOCKS + targets).astype(jnp.int32)
    tail_agg = jax.ops.segment_sum(products.reshape(-1, BLOCK, FEAT), dest_block.reshape(-1), num_segments=device_total * BLOCKS)
    combined = hub_agg + tail_agg.reshape(VERTS, FEAT)
    return jnp.maximum(jnp.dot(combined, weight, precision=highest, preferred_element_type=jnp.float32), 0.0)
```

```python
import functools

import jax
import jax.numpy as jnp
from jax import lax
from jax.experimental import pallas as pl
from jax.experimental.pallas import tpu as pltpu
from jax.sharding import PartitionSpec as P

BLOCK = 128
HALVES = 2
F32 = jnp.float32
BF16 = jnp.bfloat16


def shifted(value, axis, steps):
    count = lax.axis_size(axis)
    return lax.ppermute(value, axis, [(i, (i + steps) % count) for i in range(count)])


def swapped(value, axis, bit):
    count = lax.axis_size(axis)
    return lax.ppermute(value, axis, [(i, i ^ bit) for i in range(count)])


def split(value):
    high = value.astype(BF16)
    return high, (value - high.astype(F32)).astype(BF16)


def dot3(left, right):
    dot = functools.partial(jnp.dot, preferred_element_type=F32)
    return dot(left[0], right[0]) + (dot(left[0], right[1]) + dot(left[1], right[0]))


def vmem():
    return pl.BlockSpec(memory_space=pltpu.VMEM)


def smem():
    return pl.BlockSpec(memory_space=pltpu.SMEM)


def cost(flops, size):
    return pl.CostEstimate(flops=int(flops), bytes_accessed=int(size), transcendentals=0)


def sort_kernel(cap, blocks, count, me, reader, target, tiles, near, odd, even, own, used):
    tail_count = tiles.shape[0]
    per_block = tail_count // blocks
    for out in (near, odd, even):
        out[...] = jnp.zeros_like(out)
    blank = jnp.full((near.shape[0] - cap * BLOCK, BLOCK), -1.0, F32)
    near[cap * BLOCK :, :] = blank
    for group in range(odd.shape[0]):
        odd[group, cap * BLOCK :, :] = blank
        even[group, cap * BLOCK :, :] = blank
    own[...] = jnp.zeros_like(own)

    def clear(i, _):
        used[i] = 0
        return 0

    lax.fori_loop(0, count, clear, 0)

    def place(t, _):
        offset = lax.rem(reader[t] - me[0] + count, count)
        slot = used[offset]
        used[offset] = slot + 1
        k = t // per_block
        code = jnp.full((1, BLOCK), (target[t] * blocks + k).astype(F32), F32)
        rows = pl.ds(pl.multiple_of(slot * BLOCK, BLOCK), BLOCK)

        @pl.when(offset == 1)
        def _():
            near[rows, :] = tiles[t]
            near[pl.ds(cap * BLOCK + slot, 1), :] = code

        @pl.when(offset == 2)
        def _():
            at = (
                pl.ds(pl.multiple_of(target[t] * BLOCK, BLOCK), BLOCK),
                pl.ds(pl.multiple_of(k * BLOCK, BLOCK), BLOCK),
            )
            own[at] = own[at] + tiles[t]

        @pl.when((offset > 2) & (lax.rem(offset, 2) == 1))
        def _():
            group = (offset - 3) // 2
            odd[group, rows, :] = tiles[t]
            odd[group, pl.ds(cap * BLOCK + slot, 1), :] = code

        @pl.when((offset > 2) & (lax.rem(offset, 2) == 0))
        def _():
            group = (offset - 4) // 2
            even[group, rows, :] = tiles[t]
            even[group, pl.ds(cap * BLOCK + slot, 1), :] = code

        return 0

    lax.fori_loop(0, tail_count, place, 0)


def gathered(cap, blocks, slots):
    rows = []
    for t in range(blocks):
        row = []
        for k in range(blocks):
            total = jnp.zeros((BLOCK, BLOCK), F32)
            for j in range(cap):
                code = jnp.broadcast_to(slots[pl.ds(cap * BLOCK + j, 1), :], (BLOCK, BLOCK))
                tile = slots[pl.ds(j * BLOCK, BLOCK), :]
                total = total + jnp.where(code == float(t * blocks + k), tile, 0.0)
            row.append(total)
        rows.append(jnp.concatenate(row, 1))
    return split(jnp.concatenate(rows, 0))


def slots_kernel(cap, blocks, pairs, *refs):
    out = refs[-1]
    slots, feats, rest = refs[:pairs], refs[pairs : pairs * (1 + HALVES)], refs[pairs * (1 + HALVES) : -1]
    half = out.shape[1] // HALVES
    for p in range(pairs):
        left = gathered(cap, blocks, slots[p])
        for h in range(HALVES):
            at = (slice(None), slice(h * half, (h + 1) * half))
            value = dot3(left, split(feats[p * HALVES + h][...]))
            if p == 0:
                for addend in rest:
                    value = value + addend[at]
                out[at] = value
            else:
                out[at] = out[at] + value


def slots_product(cap, blocks, slots, feats, addends):
    rows, width = feats[0].shape[0], feats[0].shape[1] * HALVES
    args = (*slots, *feats, *addends)
    return pl.pallas_call(
        functools.partial(slots_kernel, cap, blocks, len(slots)),
        out_shape=jax.ShapeDtypeStruct((rows, width), F32),
        in_specs=[vmem()] * len(args),
        out_specs=vmem(),
        cost_estimate=cost(6 * len(slots) * rows * rows * width, 4 * sum(a.size for a in args)),
    )(*args)


def own_kernel(own, feats, out):
    out[...] = dot3(split(own[...]), split(feats[...]))


def masked(values, mask, stop, quarter, blocks):
    row_tiles = values.shape[1] // BLOCK
    rows = []
    for r in range(row_tiles):
        row = []
        for c in range(blocks):
            tile = values[0, r * BLOCK : (r + 1) * BLOCK, c * BLOCK : (c + 1) * BLOCK]
            row.append(tile * mask[stop, quarter * row_tiles + r, c].astype(F32))
        rows.append(jnp.concatenate(row, 1))
    return split(jnp.concatenate(rows, 0))


def hub_kernel(stops, blocks, order, mask, *refs):
    step = pl.program_id(0)
    values, feats = refs[: len(stops)], refs[len(stops) : 2 * len(stops)]
    rest = refs[2 * len(stops) :]
    quarter = order[step]
    total = None
    for stop, value, feat in zip(stops, values, feats):
        part = dot3(masked(value, mask, stop, quarter, blocks), split(feat[...]))
        total = part if total is None else total + part
    if len(rest) == 1:
        rest[0][0] = total
        return
    before, send, keep = rest
    total = total + before[0]

    @pl.when(step < pl.num_programs(0) // 2)
    def _():
        send[0] = total

    @pl.when(step >= pl.num_programs(0) // 2)
    def _():
        keep[0] = total


def hub_call(stops, hub_values, mask, order, feats, before=None):
    lanes = order.shape[0]
    rows, width = feats[0].shape
    blocks = rows // BLOCK
    quarter_rows = hub_values.shape[1] // lanes
    in_specs = [
        pl.BlockSpec((1, quarter_rows, rows), functools.partial(lambda s, g, o, m: (s, o[g], 0), s))
        for s in stops
    ]
    in_specs += [pl.BlockSpec((rows, width), lambda g, o, m: (0, 0)) for _ in stops]
    args = [hub_values] * len(stops) + list(feats)
    block = (1, quarter_rows, width)
    half = lanes // 2
    if before is None:
        out_specs = pl.BlockSpec(block, lambda g, o, m: (g, 0, 0))
        out_shape = jax.ShapeDtypeStruct((lanes, quarter_rows, width), F32)
    else:
        in_specs.append(pl.BlockSpec(block, lambda g, o, m: (g, 0, 0)))
        args.append(before)
        out_specs = [
            pl.BlockSpec(block, lambda g, o, m: (jnp.minimum(g, half - 1), 0, 0)),
            pl.BlockSpec(block, lambda g, o, m: (jnp.maximum(g - half, 0), 0, 0)),
        ]
        out_shape = [jax.ShapeDtypeStruct((half, quarter_rows, width), F32)] * 2
    return pl.pallas_call(
        functools.partial(hub_kernel, stops, blocks),
        out_shape=out_shape,
        grid_spec=pltpu.PrefetchScalarGridSpec(
            num_scalar_prefetch=2, grid=(lanes,), in_specs=in_specs, out_specs=out_specs
        ),
        compiler_params=pltpu.CompilerParams(dimension_semantics=("arbitrary",)),
        cost_estimate=cost(
            6 * len(stops) * lanes * quarter_rows * rows * width,
            4 * len(stops) * lanes * quarter_rows * (rows + width),
        ),
    )(order, mask, *args)


def final_kernel(parts, *refs):
    out, weight, tails = refs[-1], refs[-2], refs[: len(refs) - 2 - HALVES * parts]
    hubs = refs[len(tails) : -2]
    half = weight.shape[0] // HALVES
    total = None
    for h in range(HALVES):
        rows = slice(h * half, (h + 1) * half)
        value = tails[0][:, rows]
        for ref in tails[1:]:
            value = value + ref[:, rows]
        for ref in hubs[h * parts : (h + 1) * parts]:
            value = value + ref[...]
        part = dot3(split(value), split(weight[rows, :]))
        total = part if total is None else total + part
    out[...] = jnp.maximum(total, 0.0)


def per_device(features, weight, hub_values, hub_mask, tail_values, tail_reader, tail_target):
    rows, width = features.shape
    blk_count, lane_count = lax.axis_size("blk"), lax.axis_size("lane")
    blk, lane = lax.axis_index("blk"), lax.axis_index("lane")
    blocks = rows // BLOCK
    tail_count = tail_reader.shape[0]
    reach = blk_count // 2
    cap = (tail_count + reach - 1) // reach
    groups = reach // 2 - 1
    slot_rows = cap * BLOCK + (cap + 7) // 8 * 8
    is_odd = lax.rem(blk, 2) == 1
    half = width // HALVES
    feats = [features[:, h * half : (h + 1) * half] for h in range(HALVES)]

    below = [shifted(f, "blk", 2) for f in feats]

    near, odd, even, own = pl.pallas_call(
        functools.partial(sort_kernel, cap, blocks, blk_count),
        out_shape=[
            jax.ShapeDtypeStruct((slot_rows, BLOCK), F32),
            jax.ShapeDtypeStruct((groups, slot_rows, BLOCK), F32),
            jax.ShapeDtypeStruct((groups, slot_rows, BLOCK), F32),
            jax.ShapeDtypeStruct((rows, rows), F32),
        ],
        in_specs=[smem(), smem(), smem(), vmem()],
        out_specs=[vmem()] * 4,
        scratch_shapes=[pltpu.SMEM((blk_count,), jnp.int32)],
        cost_estimate=cost(0, 8 * tail_values.size),
    )(blk[None], tail_reader, tail_target, tail_values)

    odd_here = swapped(odd, "blk", 1)
    even_below = shifted(even, "blk", 2)
    first = jnp.where(is_odd, near, odd_here[0])[None]
    odd_below = shifted(jnp.concatenate([first, odd_here[1:]], 0), "blk", 2)

    own_part = pl.pallas_call(
        own_kernel,
        out_shape=jax.ShapeDtypeStruct((rows, width), F32),
        in_specs=[vmem()] * 2,
        out_specs=vmem(),
        cost_estimate=cost(6 * rows * rows * width, 4 * (rows * rows + 2 * rows * width)),
    )(own, features)

    masks = [m for m in range(lane_count) if m & 1][::-1] + [m for m in range(lane_count) if not m & 1][::-1]
    order = lane ^ jnp.array(masks, jnp.int32)
    before, hub_parts = [], []
    for h in range(HALVES):
        early = hub_call((0, 2), hub_values, hub_mask, order, (feats[h], below[h]))
        other = swapped(jnp.where(is_odd, below[h], feats[h]), "blk", 1)
        before.append(other)
        send, keep = hub_call((1,), hub_values, hub_mask, order, (other,), early)
        here = keep + swapped(send, "lane", 1)
        bit = 2
        while here.shape[0] > 2:
            cut = here.shape[0] // 2
            here = here[cut:] + swapped(here[:cut], "lane", bit)
            bit *= 2
        hub_parts += [here[1], swapped(here[0], "lane", bit)]

    chosen = [jnp.where(is_odd, odd_here[g], odd_below[g]) for g in range(groups)]
    running = None
    for g in reversed(range(groups)):
        addends = ([own_part] if g == 0 else []) + ([] if running is None else [running])
        part = slots_product(
            cap, blocks, (even_below[g], chosen[g]), (*below, *before), addends
        )
        running = shifted(part, "blk", 2)
    near_here = swapped(jnp.where(is_odd, odd_below[0], near), "blk", 1)
    near_part = slots_product(cap, blocks, (near_here,), before, [])

    args = (running, near_part, *hub_parts, weight)
    return pl.pallas_call(
        functools.partial(final_kernel, 2),
        out_shape=jax.ShapeDtypeStruct((rows, width), F32),
        in_specs=[vmem()] * len(args),
        out_specs=vmem(),
        cost_estimate=cost(6 * rows * width * width, 4 * sum(a.size for a in args)),
    )(*args)


def solution(mesh):
    return jax.shard_map(
        per_device,
        mesh=mesh,
        in_specs=(
            P(("blk", "lane"), None),
            P(),
            P(None, "blk", "lane"),
            P(None, "blk", "lane"),
            P(("blk", "lane"), None, None),
            P(("blk", "lane")),
            P(("blk", "lane")),
        ),
        out_specs=P(("blk", "lane"), None),
        check_vma=False,
    )
```
